32 devices in a mesh: seq: 16 (over z, y, x), head: 2 (over core).
Axes of the slice: x: 2, y: 2, z: 4, core: 2. Of those that a mesh axis runs over, the one named last changes fastest.
Arguments:
- queries: bfloat16 [1024, 1024], P('seq', 'head'), may hold values from -9 to 9
- keys: bfloat16 [2, 32768, 128], P('head', 'seq'), may hold values from -9 to 9
- values: bfloat16 [2, 32768, 128], P('head', 'seq'), may hold values from -6 to 6
- mask: int32 [8, 256], P(None, 'seq'), may hold values from 0 to 1, as said below
- out_proj: bfloat16 [1024, 4096], P('head', 'seq'), may hold values from -0.1875 to 0.1875
Outputs:
- output: bfloat16 [1024, 4096], P('seq', 'head')
The draws below stay inside these ranges and needn't reach their ends.
Inputs may be any that keep to these rules, and one draw needn't show every extreme that they name: `mask`: each entry is 0 or 1; the share of ones differs strongly between the cached positions of different seq shards.
All inputs are finite; a program needn't handle non-finite values.
Results may differ from the reference program's by a relative error of at most 0.0057.
Values may be sent and summed in bfloat16 or wider, within the bound.
No kernel may reach another device: no remote copies, remote signals or barrier semaphores. Data moves between devices by JAX's collectives and lax.ppermute only.
A program may use at most 64 MiB of HBM per device.

```python
import jax
import jax.numpy as jnp
from jax import lax

D = 4096
HD = 128
GROUP = 4
KVH = 2
QH = 8
QROWS = 1024
CACHE_DEV = 2048
KEYS = 32768
BLK = 128


def draw_mask(key, part):
    key_blocks = KEYS // BLK
    per_shard = CACHE_DEV // BLK
    shard_count = key_blocks // per_shard
    first, second = jax.random.split(jax.random.fold_in(key, 17))
    offset = jax.random.randint(second, (), 0, shard_count)
    shard = jnp.arange(key_blocks, dtype=jnp.int32) // per_shard
    level = (shard * 29 + offset) % shard_count
    threshold = 150 + 800 * level // max(shard_count - 1, 1)
    draws = jax.random.randint(first, (QROWS // BLK, key_blocks), 0, 1000)
    return (draws < threshold[None, :]).astype(jnp.int32)


def block_levels(key, dims, cuts, low, largest):
    def one(position, blocks):
        steps = jax.random.uniform(jax.random.fold_in(jax.random.fold_in(key, 6), position), (blocks,), jnp.float32, low / len(cuts), largest / len(cuts))
        return jnp.repeat(jnp.exp(steps), dims[position] // blocks).reshape((-1,) + (1,) * (len(dims) - position - 1))

    gain = one(*cuts[0])
    for cut in cuts[1:]:
        gain = gain * one(*cut)
    return gain


def gaussian(stream_key, dims, scale, limit, cuts=(), kind=jnp.bfloat16):
    array = scale * jax.random.normal(stream_key, dims, jnp.float32)
    if cuts:
        array = array * block_levels(stream_key, dims, cuts, -0.22, 0.18)
    return jnp.clip(array, -limit, limit).astype(kind)


def setup_inputs(seed: int = 0) -> dict:
    arg_keys = jax.random.split(jax.random.key(seed), 6)
    return {
        "queries": gaussian(arg_keys[0], (QROWS, QH * HD), 1.6, 9.0, ((0, 16), (1, 2))),
        "keys": gaussian(arg_keys[1], (KVH, KEYS, HD), 1.6, 9.0, ((0, 2), (1, 16))),
        "values": gaussian(arg_keys[2], (KVH, KEYS, HD), 1.0, 6.0, ((0, 2), (1, 16))),
        "mask": draw_mask(jax.random.fold_in(arg_keys[5], 71), 0),
        "out_proj": gaussian(arg_keys[4], (QH * HD, D), (QH * HD) ** -0.5, 0.1875, ((0, 2), (1, 16))),
    }


def reference(queries, keys, values, mask, out_proj):
    shards = KEYS // CACHE_DEV
    query_heads = queries.astype(jnp.float32).reshape(QROWS, KVH, GROUP, HD)
    scale = 1.0 / jnp.sqrt(jnp.float32(HD))
    offset = jnp.log(jnp.float32(KEYS))

    def one_shard(total, index):
        start = (index * CACHE_DEV).astype(jnp.int32)
        key_part = lax.dynamic_slice_in_dim(keys, start, CACHE_DEV, 1).astype(jnp.float32)
        value_part = lax.dynamic_slice_in_dim(values, start, CACHE_DEV, 1).astype(jnp.float32)
        mask_part = lax.dynamic_slice_in_dim(mask, (index * (CACHE_DEV // BLK)).astype(jnp.int32), CACHE_DEV // BLK, 1)
        live = jnp.repeat(jnp.repeat(mask_part, BLK, axis=0), BLK, axis=1) > 0
        score = jnp.einsum('qhgd,hkd->hgqk', query_heads, key_part) * scale - offset
        weight = jnp.where(live[None, None], jax.nn.sigmoid(score), 0.0).astype(jnp.bfloat16)
        weight = lax.optimization_barrier(weight).astype(jnp.float32)
        return (total + jnp.einsum('hgqk,hkd->qhgd', weight, value_part), None)
    start_total = jnp.zeros((QROWS, KVH, GROUP, HD), jnp.float32)
    attended, unused = lax.scan(one_shard, start_total, jnp.arange(shards, dtype=jnp.int32))
    attended_bf = attended.reshape(QROWS, QH * HD).astype(jnp.bfloat16)
    return jnp.dot(attended_bf, out_proj, preferred_element_type=jnp.float32).astype(jnp.bfloat16)
```

```python
import functools
import math

import jax
import jax.numpy as jnp
from jax import lax
from jax.experimental import pallas as pl
from jax.experimental.pallas import tpu as pltpu
from jax.sharding import PartitionSpec as P

BLK = 128
TILE = 256
LOG2E = math.log2(math.e)
BOTH = ("seq", "head")


def attend_kernel(sources, total_keys, own_rows, flip, has_acc, *refs):
    masks, refs = refs[:sources], refs[sources:]
    q_ref, refs = refs[0], refs[1:]
    keys, refs = refs[:sources], refs[sources:]
    values, refs = refs[:sources], refs[sources:]
    if has_acc:
        acc_in, refs = refs[0], refs[1:]
    out_ref, stacked, total = refs
    rows, width = q_ref.shape
    cached, head_size = keys[0].shape
    group = width // head_size
    blocks = rows // own_rows
    part = group * own_rows
    tile = min(TILE, cached)
    scale = -LOG2E / math.sqrt(head_size)
    offset = math.log(total_keys) * LOG2E
    seq = lax.axis_index("seq")
    plane = lax.rem(seq, 4)
    line = lax.div(seq, 4)
    odd = lax.rem(lax.axis_index("head"), 2)
    plane = plane ^ jnp.where(odd == 1, flip[1], flip[0])
    mask_rows = [((line ^ j) * 4 + plane) * own_rows // BLK for j in range(blocks)]
    for j in range(blocks):
        for i in range(group):
            stacked[j * part + i * own_rows : j * part + (i + 1) * own_rows, :] = q_ref[
                j * own_rows : (j + 1) * own_rows, i * head_size : (i + 1) * head_size
            ]
    lanes = lax.broadcasted_iota(jnp.int32, (1, tile), 1) // BLK
    first = True
    for mask_ref, k_ref, v_ref in zip(masks, keys, values):
        for t in range(cached // tile):
            score = lax.dot_general(
                stacked[...],
                k_ref[t * tile : (t + 1) * tile, :],
                (((1,), (1,)), ((), ())),
                preferred_element_type=jnp.float32,
            )
            weights = []
            for j in range(blocks):
                bias = jnp.full((1, tile), offset, jnp.float32)
                for c in range(tile // BLK):
                    live = mask_ref[mask_rows[j], t * (tile // BLK) + c] > 0
                    bias = jnp.where(lanes == c, jnp.where(live, offset, 1e30).astype(jnp.float32), bias)
                grown = jnp.exp2(score[j * part : (j + 1) * part] * scale + bias)
                weights.append((1.0 / (1.0 + grown)).astype(jnp.bfloat16))
            weight = jnp.concatenate(weights, axis=0)
            term = jnp.dot(weight, v_ref[t * tile : (t + 1) * tile, :], preferred_element_type=jnp.float32)
            total[...] = term if first else total[...] + term
            first = False
    for j in range(blocks):
        for i in range(group):
            here = (slice(j * own_rows, (j + 1) * own_rows), slice(i * head_size, (i + 1) * head_size))
            value = total[j * part + i * own_rows : j * part + (i + 1) * own_rows, :]
            if has_acc:
                value = value + acc_in[here]
            out_ref[here] = value.astype(out_ref.dtype)


def attend(q, sources, total_keys, own_rows, flip, acc, dtype):
    rows, width = q.shape
    cached, head_size = sources[0][1].shape
    count = len(sources)
    arrays = (
        [s[0] for s in sources] + [q] + [s[1] for s in sources] + [s[2] for s in sources] + ([] if acc is None else [acc])
    )
    vmem = pl.BlockSpec(memory_space=pltpu.VMEM)
    smem = pl.BlockSpec(memory_space=pltpu.SMEM)
    scores = rows * (width // head_size) * cached * count
    return pl.pallas_call(
        functools.partial(attend_kernel, count, total_keys, own_rows, flip, acc is not None),
        out_shape=jax.ShapeDtypeStruct((rows, width), dtype),
        in_specs=[smem] * count + [vmem] * (len(arrays) - count),
        out_specs=vmem,
        scratch_shapes=[
            pltpu.VMEM((rows * width // head_size, head_size), jnp.bfloat16),
            pltpu.VMEM((rows * width // head_size, head_size), jnp.float32),
        ],
        cost_estimate=pl.CostEstimate(
            flops=4 * scores * head_size, transcendentals=2 * scores, bytes_accessed=4 * count * cached * head_size
        ),
    )(*arrays)


def on_device(queries, keys, values, mask, out_proj):
    seq_size, heads = lax.axis_size("seq"), lax.axis_size("head")
    lines = seq_size // 4
    per_head = lines // heads
    own_rows = queries.shape[0]
    columns = out_proj.shape[1]
    total_keys = keys.shape[1] * seq_size
    seq, head = lax.axis_index("seq"), lax.axis_index("head")
    line, plane = seq // 4, seq % 4

    def move(x, target):
        pairs = []
        for s in range(seq_size):
            for h in range(heads):
                z, p, g = target(s // 4, s % 4, h)
                pairs.append((s * heads + h, (z * 4 + p) * heads + g))
        return lax.ppermute(x, BOTH, pairs)

    def pair(x):
        return move(x, lambda z, p, h: (z, p ^ (1 + h % 2), h))

    def other(x):
        return move(x, lambda z, p, h: (z, p ^ (2 - h % 2), h))

    key_own, value_own = keys[0], values[0]
    lined = [queries] + [move(queries, lambda z, p, h, k=k: (z ^ k, p, h)) for k in range(1, lines)]
    key_pair, value_pair, mask_pair = pair(key_own), pair(value_own), pair(mask)
    q_own = jnp.concatenate(lined, axis=0)
    q_other = other(q_own)

    weights = []
    for r in range(lines):
        pairs = []
        for s in range(seq_size):
            for h in range(heads):
                m = (s // 4) ^ r
                source = ((h * per_head + m // heads) * 4 + s % 4) * heads + m % heads
                pairs.append((source, s * heads + h))
        weights.append(lax.ppermute(out_proj, BOTH, pairs))
    stack = jnp.stack(weights)
    proj = jnp.concatenate(
        [
            jnp.concatenate(
                [
                    lax.dynamic_index_in_dim(stack, (i * heads + (head ^ k)) ^ line, 0, keepdims=False)
                    for i in range(per_head)
                ],
                axis=1,
            )
            for k in range(heads)
        ],
        axis=0,
    )

    near, far = (mask, key_own, value_own), (mask_pair, key_pair, value_pair)
    part = attend(q_own, [near], total_keys, own_rows, (0, 0), None, jnp.float32)
    share = attend(q_other, [near, far], total_keys, own_rows, (2, 1), None, jnp.bfloat16)
    share = other(share)
    part = attend(q_own, [far], total_keys, own_rows, (0, 0), part, jnp.float32)
    total = part + share.astype(jnp.float32)

    sums = total[:own_rows]
    blocks = total.astype(jnp.bfloat16)
    for k in range(1, lines):
        block = blocks[k * own_rows : (k + 1) * own_rows]
        sums = sums + move(block, lambda z, p, h, k=k: (z ^ k, p, h)).astype(jnp.float32)
    attended = sums.astype(jnp.bfloat16)

    quad = [attended] + [move(attended, lambda z, p, h, k=k: (z, p ^ k, h)) for k in range(1, 4)]
    quad = jnp.concatenate(quad, axis=0)
    width = quad.shape[1]
    terms = jnp.dot(quad, proj[:width], preferred_element_type=jnp.float32)
    for k in range(1, heads):
        there = move(quad, lambda z, p, h, k=k: (z, p, h ^ k))
        terms = terms + jnp.dot(there, proj[k * width : (k + 1) * width], preferred_element_type=jnp.float32)
    result = terms.astype(jnp.bfloat16)

    got = [result[:own_rows]] + [
        move(result[k * own_rows : (k + 1) * own_rows], lambda z, p, h, k=k: (z, p ^ k, h)) for k in range(1, 4)
    ]
    low, high = plane % 2 == 1, plane // 2 == 1
    got = [jnp.where(low, got[k ^ 1], got[k]) for k in range(4)]
    got = [jnp.where(high, got[k ^ 2], got[k]) for k in range(4)]
    return jnp.concatenate(
        [got[p][:, i * columns : (i + 1) * columns] for i in range(per_head) for p in range(4)], axis=1
    )


def solution(mesh):
    placed = (
        P("seq", "head"),
        P("head", "seq", None),
        P("head", "seq", None),
        P(None, "seq"),
        P("head", "seq"),
    )
    return jax.shard_map(
        on_device, mesh=mesh, in_specs=placed, out_specs=P("seq", "head"), check_vma=False
    )
```

```python
import functools
import math

import jax
import jax.numpy as jnp
from jax import lax
from jax.experimental import pallas as pl
from jax.experimental.pallas import tpu as pltpu
from jax.sharding import PartitionSpec as P


BLK = 128
TILE = 256
CHUNK = 512
VMEM_LIMIT = 24 * 1024 * 1024
LOG2E = math.log2(math.e)
BOTH = ("seq", "head")


def attend_kernel(sources, total_keys, own_rows, flip, has_acc, *refs):
    masks, refs = refs[:sources], refs[sources:]
    q_ref, refs = refs[0], refs[1:]
    keys, refs = refs[:sources], refs[sources:]
    values, refs = refs[:sources], refs[sources:]
    if has_acc:
        acc_in, refs = refs[0], refs[1:]
    out_ref, refs = refs[0], refs[1:]
    if has_acc:
        out_here, refs = refs[0], refs[1:]
    q_here, stacked, total, key_here, value_here, sems = refs
    rows, width = q_ref.shape
    cached, head_size = keys[0].shape
    group = width // head_size
    blocks = rows // own_rows
    part = group * own_rows
    tile = min(TILE, cached)
    chunk = min(CHUNK, cached)
    chunks = cached // chunk
    scale = -LOG2E / math.sqrt(head_size)
    offset = math.log(total_keys) * LOG2E

    loads = [pltpu.make_async_copy(q_ref, q_here, sems.at[0])]
    for n in range(sources):
        for c in range(chunks):
            span = pl.ds(c * chunk, chunk)
            for array, (far, here) in enumerate(((keys[n], key_here), (values[n], value_here))):
                loads.append(
                    pltpu.make_async_copy(
                        far.at[span, :], here.at[n, span, :], sems.at[1 + (n * chunks + c) * 2 + array]
                    )
                )
    if has_acc:
        loads.append(pltpu.make_async_copy(acc_in, out_here, sems.at[1 + sources * chunks * 2]))
    for load in loads:
        load.start()

    seq = lax.axis_index("seq")
    plane = lax.rem(seq, 4)
    line = lax.div(seq, 4)
    odd = lax.rem(lax.axis_index("head"), 2)
    plane = plane ^ jnp.where(odd == 1, flip[1], flip[0])
    mask_rows = [((line ^ j) * 4 + plane) * own_rows // BLK for j in range(blocks)]
    loads[0].wait()
    for j in range(blocks):
        for i in range(group):
            stacked[j * part + i * own_rows : j * part + (i + 1) * own_rows, :] = q_here[
                j * own_rows : (j + 1) * own_rows, i * head_size : (i + 1) * head_size
            ]
    lanes = lax.broadcasted_iota(jnp.int32, (1, tile), 1) // BLK
    first = True
    for n in range(sources):
        for t in range(cached // tile):
            if t * tile % chunk == 0:
                at = 1 + (n * chunks + t * tile // chunk) * 2
                loads[at].wait()
                loads[at + 1].wait()
            score = lax.dot_general(
                stacked[...],
                key_here[n, t * tile : (t + 1) * tile, :],
                (((1,), (1,)), ((), ())),
                preferred_element_type=jnp.float32,
            )
            weights = []
            for j in range(blocks):
                bias = jnp.full((1, tile), offset, jnp.float32)
                for c in range(tile // BLK):
                    live = masks[n][mask_rows[j], t * (tile // BLK) + c] > 0
                    bias = jnp.where(lanes == c, jnp.where(live, offset, 1e30).astype(jnp.float32), bias)
                grown = jnp.exp2(score[j * part : (j + 1) * part] * scale + bias)
                weights.append((1.0 / (1.0 + grown)).astype(jnp.bfloat16))
            weight = jnp.concatenate(weights, axis=0)
            term = jnp.dot(weight, value_here[n, t * tile : (t + 1) * tile, :], preferred_element_type=jnp.float32)
            total[...] = term if first else total[...] + term
            first = False
    if has_acc:
        loads[-1].wait()
    for j in range(blocks):
        for i in range(group):
            here = (slice(j * own_rows, (j + 1) * own_rows), slice(i * head_size, (i + 1) * head_size))
            value = total[j * part + i * own_rows : j * part + (i + 1) * own_rows, :]
            if has_acc:
                value = value + out_here[here]
            out_ref[here] = value.astype(out_ref.dtype)


def attend(q, sources, total_keys, own_rows, flip, acc, dtype):
    rows, width = q.shape
    cached, head_size = sources[0][1].shape
    count = len(sources)
    arrays = (
        [s[0] for s in sources] + [q] + [s[1] for s in sources] + [s[2] for s in sources] + ([] if acc is None else [acc])
    )
    anywhere = pl.BlockSpec(memory_space=pl.ANY)
    smem = pl.BlockSpec(memory_space=pltpu.SMEM)
    scores = rows * (width // head_size) * cached * count
    chunks = cached // min(CHUNK, cached)
    return pl.pallas_call(
        functools.partial(attend_kernel, count, total_keys, own_rows, flip, acc is not None),
        out_shape=jax.ShapeDtypeStruct((rows, width), dtype),
        in_specs=[smem] * count + [anywhere] * (len(arrays) - count),
        out_specs=pl.BlockSpec(memory_space=pltpu.VMEM),
        scratch_shapes=([] if acc is None else [pltpu.VMEM((rows, width), jnp.float32)])
        + [
            pltpu.VMEM((rows, width), jnp.bfloat16),
            pltpu.VMEM((rows * width // head_size, head_size), jnp.bfloat16),
            pltpu.VMEM((rows * width // head_size, head_size), jnp.float32),
            pltpu.VMEM((count, cached, head_size), jnp.bfloat16),
            pltpu.VMEM((count, cached, head_size), jnp.bfloat16),
            pltpu.SemaphoreType.DMA((2 + count * chunks * 2,)),
        ],
        compiler_params=pltpu.CompilerParams(vmem_limit_bytes=VMEM_LIMIT),
        cost_estimate=pl.CostEstimate(
            flops=4 * scores * head_size, transcendentals=2 * scores, bytes_accessed=4 * count * cached * head_size
        ),
    )(*arrays)


def small_call(kernel, out_shapes, args, flops=0):
    vmem = pl.BlockSpec(memory_space=pltpu.VMEM)
    return pl.pallas_call(
        kernel,
        out_shape=out_shapes,
        in_specs=[vmem] * len(args),
        out_specs=jax.tree.map(lambda _: vmem, out_shapes),
        compiler_params=pltpu.CompilerParams(vmem_limit_bytes=VMEM_LIMIT),
        cost_estimate=pl.CostEstimate(flops=flops, transcendentals=0, bytes_accessed=1 << 20),
    )(*args)


def merge_kernel(part_ref, share_ref, own_ref, *block_refs):
    own_rows = own_ref.shape[0]
    for k in range(len(block_refs) + 1):
        rows = slice(k * own_rows, (k + 1) * own_rows)
        value = part_ref[rows, :] + share_ref[rows, :].astype(jnp.float32)
        if k == 0:
            own_ref[...] = value
        else:
            block_refs[k - 1][...] = value.astype(jnp.bfloat16)


def project_kernel(heads, *refs):
    inputs, refs = refs[:heads], refs[heads:]
    blocks, outs = refs[:-4], refs[-4:]
    own_rows = outs[0].shape[0]
    width = inputs[0].shape[1]
    columns = blocks[0].shape[1]
    for m, block in enumerate(blocks):
        value = None
        for k in range(heads):
            term = jnp.dot(
                inputs[k][...], block[k * width : (k + 1) * width, :], preferred_element_type=jnp.float32
            )
            value = term if value is None else value + term
        value = value.astype(jnp.bfloat16)
        for k in range(4):
            outs[k][:, m * columns : (m + 1) * columns] = value[k * own_rows : (k + 1) * own_rows]


def place_kernel(per_head, *refs):
    got, out_ref = refs[:4], refs[4]
    columns = got[0].shape[1] // per_head
    seq = lax.axis_index("seq")
    plane, line = lax.rem(seq, 4), lax.div(seq, 4)
    pieces = [[g[:, m * columns : (m + 1) * columns] for m in range(per_head)] for g in got]
    bit = 1
    while bit < 4:
        here = lax.rem(lax.div(plane, bit), 2) == 1
        pieces = [[jnp.where(here, b, a) for a, b in zip(pieces[k], pieces[k ^ bit])] for k in range(4)]
        bit *= 2
    bit = 1
    while bit < per_head:
        here = lax.rem(lax.div(line, bit), 2) == 1
        pieces = [[jnp.where(here, row[m ^ bit], row[m]) for m in range(per_head)] for row in pieces]
        bit *= 2
    for m in range(per_head):
        for p in range(4):
            at = (m * 4 + p) * columns
            out_ref[:, at : at + columns] = pieces[p][m]


def on_device(queries, keys, values, mask, out_proj):
    seq_size, heads = lax.axis_size("seq"), lax.axis_size("head")
    lines = seq_size // 4
    per_head = lines // heads
    own_rows = queries.shape[0]
    columns = out_proj.shape[1]
    total_keys = keys.shape[1] * seq_size
    seq = lax.axis_index("seq")
    line = seq // 4
    home = line // per_head == lax.axis_index("head")

    def move(x, target):
        pairs = []
        for s in range(seq_size):
            for h in range(heads):
                to = target(s // 4, s % 4, h)
                if to is not None:
                    pairs.append((s * heads + h, (to[0] * 4 + to[1]) * heads + to[2]))
        return lax.ppermute(x, BOTH, pairs)

    def pair(x):
        return move(x, lambda z, p, h: (z, p ^ (1 + h % 2), h))

    def other(x):
        return move(x, lambda z, p, h: (z, p ^ (2 - h % 2), h))

    def along(x, k):
        return move(x, lambda z, p, h: (z ^ k, p, h))

    def inside(x, k):
        return move(x, lambda z, p, h: (z, p ^ k, h))

    def across(x, k):
        return move(x, lambda z, p, h: (z, p, h ^ k))

    key_own, value_own = keys[0], values[0]
    lined = [queries] + [along(queries, k) for k in range(1, lines)]
    mask_pair, key_pair, value_pair = pair(mask), pair(key_own), pair(value_own)
    q_own = jnp.concatenate(lined, axis=0)
    q_other = other(q_own)

    rows_all = jnp.concatenate([out_proj] + [across(out_proj, k) for k in range(1, heads)], axis=0)
    spread = None
    for k in range(per_head, lines, per_head):
        got = move(rows_all, lambda z, p, h, k=k: (z ^ k, p, h) if z // per_head == h else None)
        spread = got if spread is None else spread + got
    proj_here = rows_all if spread is None else jnp.where(home, rows_all, spread)
    proj = [proj_here] + [along(proj_here, k) for k in range(1, per_head)]

    near, far = (mask, key_own, value_own), (mask_pair, key_pair, value_pair)
    part = attend(q_own, [near], total_keys, own_rows, (0, 0), None, jnp.float32)
    share = attend(q_other, [near, far], total_keys, own_rows, (2, 1), None, jnp.bfloat16)
    share = other(share)
    part = attend(q_own, [far], total_keys, own_rows, (0, 0), part, jnp.float32)
    width = part.shape[1]
    block = jax.ShapeDtypeStruct((own_rows, width), jnp.bfloat16)
    merged = small_call(
        merge_kernel, [jax.ShapeDtypeStruct((own_rows, width), jnp.float32)] + [block] * (lines - 1), [part, share]
    )
    sums = merged[0]
    for k in range(1, lines):
        sums = sums + along(merged[k], k).astype(jnp.float32)
    attended = sums.astype(jnp.bfloat16)

    quad = jnp.concatenate([attended] + [inside(attended, k) for k in range(1, 4)], axis=0)
    full = [quad] + [across(quad, k) for k in range(1, heads)]
    piece = jax.ShapeDtypeStruct((own_rows, per_head * columns), jnp.bfloat16)
    result = small_call(
        functools.partial(project_kernel, heads),
        [piece] * 4,
        full + proj,
        flops=8 * own_rows * heads * width * per_head * columns,
    )
    got = [result[0]] + [inside(result[k], k) for k in range(1, 4)]
    return small_call(
        functools.partial(place_kernel, per_head),
        jax.ShapeDtypeStruct((own_rows, 4 * per_head * columns), jnp.bfloat16),
        got,
    )


def solution(mesh):
    placed = (
        P("seq", "head"),
        P("head", "seq", None),
        P("head", "seq", None),
        P(None, "seq"),
        P("head", "seq"),
    )

    return jax.shard_map(on_device, mesh=mesh, in_specs=placed, out_specs=P("seq", "head"), check_vma=False)
```

```python
import functools
import math

import jax
import jax.numpy as jnp
from jax import lax
from jax.experimental import pallas as pl
from jax.experimental.pallas import tpu as pltpu
from jax.sharding import PartitionSpec as P


BLK = 128
TILE = 256
VMEM_LIMIT = 24 * 1024 * 1024
LOG2E = math.log2(math.e)
BOTH = ("seq", "head")


def attend_kernel(own_rows, flip, has_acc, bias_ref, q_ref, k_ref, v_ref, *refs):
    if has_acc:
        acc_in, refs = refs[0], refs[1:]
    out_ref, stacked, total = refs
    rows, width = q_ref.shape
    cached, head_size = k_ref.shape
    group = width // head_size
    blocks = rows // own_rows
    part = group * own_rows
    tile = min(TILE, cached)
    scale = -LOG2E / math.sqrt(head_size)
    seq = lax.axis_index("seq")
    plane = lax.rem(seq, 4)
    line = lax.div(seq, 4)
    odd = lax.rem(lax.axis_index("head"), 2)
    plane = plane ^ jnp.where(odd == 1, flip[1], flip[0])
    biases = []
    for j in range(blocks):
        mask_row = ((line ^ j) * 4 + plane) * own_rows // BLK
        biases.append(bias_ref[pl.ds(mask_row, 1), :])
    for j in range(blocks):
        for i in range(group):
            stacked[j * part + i * own_rows : j * part + (i + 1) * own_rows, :] = q_ref[
                j * own_rows : (j + 1) * own_rows, i * head_size : (i + 1) * head_size
            ]
    for t in range(cached // tile):
        score = lax.dot_general(
            stacked[...],
            k_ref[t * tile : (t + 1) * tile, :],
            (((1,), (1,)), ((), ())),
            preferred_element_type=jnp.float32,
        )
        weights = []
        for j in range(blocks):
            bias = jnp.concatenate(
                [
                    jnp.broadcast_to(biases[j][:, c : c + 1], (1, BLK))
                    for c in range(t * (tile // BLK), (t + 1) * (tile // BLK))
                ],
                axis=1,
            )
            grown = jnp.exp2(score[j * part : (j + 1) * part] * scale + bias)
            weights.append((1.0 / (1.0 + grown)).astype(jnp.bfloat16))
        weight = jnp.concatenate(weights, axis=0)
        term = jnp.dot(weight, v_ref[t * tile : (t + 1) * tile, :], preferred_element_type=jnp.float32)
        total[...] = term if t == 0 else total[...] + term
    for j in range(blocks):
        for i in range(group):
            here = (slice(j * own_rows, (j + 1) * own_rows), slice(i * head_size, (i + 1) * head_size))
            value = total[j * part + i * own_rows : j * part + (i + 1) * own_rows, :]
            if has_acc:
                value = value + acc_in[here]
            out_ref[here] = value.astype(out_ref.dtype)


def attend(q, source, own_rows, flip, acc, dtype):
    rows, width = q.shape
    cached, head_size = source[1].shape
    stacked = (rows * width // head_size, head_size)
    scores = stacked[0] * cached
    vmem = pl.BlockSpec(memory_space=pltpu.VMEM)
    args = [source[0], q, source[1], source[2]] + ([] if acc is None else [acc])
    return pl.pallas_call(
        functools.partial(attend_kernel, own_rows, flip, acc is not None),
        out_shape=jax.ShapeDtypeStruct((rows, width), dtype),
        in_specs=[vmem] * len(args),
        out_specs=vmem,
        scratch_shapes=[pltpu.VMEM(stacked, jnp.bfloat16), pltpu.VMEM(stacked, jnp.float32)],
        compiler_params=pltpu.CompilerParams(vmem_limit_bytes=VMEM_LIMIT),
        cost_estimate=pl.CostEstimate(
            flops=4 * scores * head_size, transcendentals=2 * scores, bytes_accessed=4 * cached * head_size
        ),
    )(*args)


def small_call(kernel, out_shapes, args, flops=0):
    vmem = pl.BlockSpec(memory_space=pltpu.VMEM)
    return pl.pallas_call(
        kernel,
        out_shape=out_shapes,
        in_specs=[vmem] * len(args),
        out_specs=jax.tree.map(lambda _: vmem, out_shapes),
        compiler_params=pltpu.CompilerParams(vmem_limit_bytes=VMEM_LIMIT),
        cost_estimate=pl.CostEstimate(flops=flops, transcendentals=0, bytes_accessed=1 << 20),
    )(*args)


def stage_kernel(key_far, value_far, key_here, value_here, sems):
    copies = [
        pltpu.make_async_copy(far, here, sems.at[i])
        for i, (far, here) in enumerate(((key_far, key_here), (value_far, value_here)))
    ]
    for copy in copies:
        copy.start()
    for copy in copies:
        copy.wait()


def stage(keys, values):
    vmem = pl.BlockSpec(memory_space=pltpu.VMEM)
    return pl.pallas_call(
        stage_kernel,
        name="stage",
        out_shape=[jax.ShapeDtypeStruct(x.shape, x.dtype) for x in (keys, values)],
        in_specs=[pl.BlockSpec(memory_space=pl.ANY)] * 2,
        out_specs=[vmem] * 2,
        scratch_shapes=[pltpu.SemaphoreType.DMA((2,))],
        compiler_params=pltpu.CompilerParams(vmem_limit_bytes=VMEM_LIMIT),
        cost_estimate=pl.CostEstimate(flops=0, transcendentals=0, bytes_accessed=4 * keys.size),
    )(keys, values)


def merge_kernel(part_ref, share_ref, own_ref, *block_refs):
    own_rows = own_ref.shape[0]
    for k in range(len(block_refs) + 1):
        rows = slice(k * own_rows, (k + 1) * own_rows)
        value = part_ref[rows, :] + share_ref[rows, :].astype(jnp.float32)
        if k == 0:
            own_ref[...] = value
        else:
            block_refs[k - 1][...] = value.astype(jnp.bfloat16)


def project_kernel(heads, *refs):
    inputs, refs = refs[:heads], refs[heads:]
    blocks, outs = refs[:-4], refs[-4:]
    own_rows = outs[0].shape[0]
    width = inputs[0].shape[1]
    columns = blocks[0].shape[1]
    for m, block in enumerate(blocks):
        value = None
        for k in range(heads):
            term = jnp.dot(
                inputs[k][...], block[k * width : (k + 1) * width, :], preferred_element_type=jnp.float32
            )
            value = term if value is None else value + term
        value = value.astype(jnp.bfloat16)
        for k in range(4):
            outs[k][:, m * columns : (m + 1) * columns] = value[k * own_rows : (k + 1) * own_rows]


def place_kernel(per_head, *refs):
    got, out_ref = refs[:4], refs[4]
    columns = got[0].shape[1] // per_head
    seq = lax.axis_index("seq")
    plane, line = lax.rem(seq, 4), lax.div(seq, 4)
    pieces = [[g[:, m * columns : (m + 1) * columns] for m in range(per_head)] for g in got]
    bit = 1
    while bit < 4:
        here = lax.rem(lax.div(plane, bit), 2) == 1
        pieces = [[jnp.where(here, b, a) for a, b in zip(pieces[k], pieces[k ^ bit])] for k in range(4)]
        bit *= 2
    bit = 1
    while bit < per_head:
        here = lax.rem(lax.div(line, bit), 2) == 1
        pieces = [[jnp.where(here, row[m ^ bit], row[m]) for m in range(per_head)] for row in pieces]
        bit *= 2
    for m in range(per_head):
        for p in range(4):
            at = (m * 4 + p) * columns
            out_ref[:, at : at + columns] = pieces[p][m]


def on_device(queries, keys, values, mask, out_proj):
    seq_size, heads = lax.axis_size("seq"), lax.axis_size("head")
    lines = seq_size // 4
    per_head = lines // heads
    own_rows = queries.shape[0]
    columns = out_proj.shape[1]
    total_keys = keys.shape[1] * seq_size
    line, head = lax.axis_index("seq") // 4, lax.axis_index("head")

    def move(x, target):
        pairs = []
        for s in range(seq_size):
            for h in range(heads):
                to = target(s // 4, s % 4, h)
                if to is not None:
                    pairs.append((s * heads + h, (to[0] * 4 + to[1]) * heads + to[2]))
        return lax.ppermute(x, BOTH, pairs)

    def pair(x):
        return move(x, lambda z, p, h: (z, p ^ (1 + h % 2), h))

    def other(x):
        return move(x, lambda z, p, h: (z, p ^ (2 - h % 2), h))

    def along(x, k):
        return move(x, lambda z, p, h: (z ^ k, p, h))

    def inside(x, k):
        return move(x, lambda z, p, h: (z, p ^ k, h))

    def across(x, k):
        return move(x, lambda z, p, h: (z, p, h ^ k))

    key_own, value_own = keys[0], values[0]
    lined = [queries] + [along(queries, k) for k in range(1, lines)]
    bias = jnp.where(mask > 0, jnp.float32(math.log(total_keys) * LOG2E), jnp.float32(1e30))
    bias_pair, key_pair, value_pair = pair(bias), pair(key_own), pair(value_own)
    q_own = jnp.concatenate(lined, axis=0)
    q_other = other(q_own)

    held, step = [out_proj], per_head
    while step < lines:
        held += [along(block, step) for block in held]
        step *= 2
    bit = 1
    while bit < heads:
        here = ((line // per_head) ^ head) // bit % 2 == 1
        held = [jnp.where(here, held[i ^ bit], held[i]) for i in range(heads)]
        bit *= 2
    rows_all = jnp.concatenate([held[0]] + [across(held[k], k) for k in range(1, heads)], axis=0)
    proj = [rows_all] + [along(rows_all, k) for k in range(1, per_head)]

    near, far = (bias, *stage(key_own, value_own)), (bias_pair, key_pair, value_pair)

    def attention(q, source, flip, acc, dtype=jnp.float32):
        return attend(q, source, own_rows, flip, acc, dtype)

    part = attention(q_own, near, (0, 0), None)
    share = attention(q_other, near, (2, 1), None)
    share = other(attention(q_other, far, (2, 1), share, jnp.bfloat16))
    part = attention(q_own, far, (0, 0), part)
    width = part.shape[1]
    block = jax.ShapeDtypeStruct((own_rows, width), jnp.bfloat16)
    merged = small_call(
        merge_kernel, [jax.ShapeDtypeStruct((own_rows, width), jnp.float32)] + [block] * (lines - 1), [part, share]
    )
    sums = merged[0]
    for k in range(1, lines):
        sums = sums + along(merged[k], k).astype(jnp.float32)
    attended = sums.astype(jnp.bfloat16)

    quad = jnp.concatenate([attended] + [inside(attended, k) for k in range(1, 4)], axis=0)
    full = [quad] + [across(quad, k) for k in range(1, heads)]
    piece = jax.ShapeDtypeStruct((own_rows, per_head * columns), jnp.bfloat16)
    result = small_call(
        functools.partial(project_kernel, heads),
        [piece] * 4,
        full + proj,
        flops=8 * own_rows * heads * width * per_head * columns,
    )
    got = [result[0]] + [inside(result[k], k) for k in range(1, 4)]
    return small_call(
        functools.partial(place_kernel, per_head),
        jax.ShapeDtypeStruct((own_rows, 4 * per_head * columns), jnp.bfloat16),
        got,
    )


def solution(mesh):
    placed = (
        P("seq", "head"),
        P("head", "seq", None),
        P("head", "seq", None),
        P(None, "seq"),
        P("head", "seq"),
    )

    return jax.shard_map(on_device, mesh=mesh, in_specs=placed, out_specs=P("seq", "head"), check_vma=False)
```

```python
import functools
import math

import jax
import jax.numpy as jnp
from jax import lax
from jax.experimental import pallas as pl
from jax.experimental.pallas import tpu as pltpu
from jax.sharding import PartitionSpec as P


BLK = 128
TILE = 256
VMEM_LIMIT = 24 * 1024 * 1024
LOG2E = math.log2(math.e)
BOTH = ("seq", "head")


def attend_kernel(own_rows, flip, members, sources, has_acc, q_ref, *refs):
    given, refs = refs[: 3 * sources], refs[3 * sources :]
    if has_acc:
        acc_in, refs = refs[0], refs[1:]
    out_ref, stacked, total = refs
    width = q_ref.shape[1]
    cached, head_size = given[1].shape
    group = width // head_size
    part = group * own_rows
    tile = min(TILE, cached)
    scale = -LOG2E / math.sqrt(head_size)
    seq = lax.axis_index("seq")
    plane = lax.rem(seq, 4)
    line = lax.div(seq, 4)
    odd = lax.rem(lax.axis_index("head"), 2)
    plane = plane ^ jnp.where(odd == 1, flip[1], flip[0])
    for j, member in enumerate(members):
        for i in range(group):
            stacked[j * part + i * own_rows : j * part + (i + 1) * own_rows, :] = q_ref[
                member * own_rows : (member + 1) * own_rows, i * head_size : (i + 1) * head_size
            ]
    for n in range(sources):
        bias_ref, k_ref, v_ref = given[3 * n : 3 * n + 3]
        biases = []
        for member in members:
            mask_row = ((line ^ member) * 4 + plane) * own_rows // BLK
            biases.append(bias_ref[pl.ds(mask_row, 1), :])
        for t in range(cached // tile):
            score = lax.dot_general(
                stacked[...],
                k_ref[t * tile : (t + 1) * tile, :],
                (((1,), (1,)), ((), ())),
                preferred_element_type=jnp.float32,
            )
            weights = []
            for j in range(len(members)):
                bias = jnp.concatenate(
                    [
                        jnp.broadcast_to(biases[j][:, c : c + 1], (1, BLK))
                        for c in range(t * (tile // BLK), (t + 1) * (tile // BLK))
                    ],
                    axis=1,
                )
                grown = jnp.exp2(score[j * part : (j + 1) * part] * scale + bias)
                weights.append((1.0 / (1.0 + grown)).astype(jnp.bfloat16))
            weight = jnp.concatenate(weights, axis=0)
            term = jnp.dot(weight, v_ref[t * tile : (t + 1) * tile, :], preferred_element_type=jnp.float32)
            total[...] = term if n == 0 and t == 0 else total[...] + term
    for j in range(len(members)):
        for i in range(group):
            here = (slice(j * own_rows, (j + 1) * own_rows), slice(i * head_size, (i + 1) * head_size))
            value = total[j * part + i * own_rows : j * part + (i + 1) * own_rows, :]
            if has_acc:
                value = value + acc_in[here]
            out_ref[here] = value.astype(out_ref.dtype)


def attend(q, sources, own_rows, flip, members, acc, dtype):
    width = q.shape[1]
    cached, head_size = sources[0][1].shape
    rows = len(members) * own_rows
    stacked = (rows * width // head_size, head_size)
    scores = stacked[0] * cached * len(sources)
    vmem = pl.BlockSpec(memory_space=pltpu.VMEM)
    args = [q] + [x for source in sources for x in source] + ([] if acc is None else [acc])
    return pl.pallas_call(
        functools.partial(attend_kernel, own_rows, flip, members, len(sources), acc is not None),
        out_shape=jax.ShapeDtypeStruct((rows, width), dtype),
        in_specs=[vmem] * len(args),
        out_specs=vmem,
        scratch_shapes=[pltpu.VMEM(stacked, jnp.bfloat16), pltpu.VMEM(stacked, jnp.float32)],
        compiler_params=pltpu.CompilerParams(vmem_limit_bytes=VMEM_LIMIT),
        cost_estimate=pl.CostEstimate(
            flops=4 * scores * head_size, transcendentals=2 * scores, bytes_accessed=4 * cached * head_size
        ),
    )(*args)


def small_call(kernel, out_shapes, args, flops=0):
    vmem = pl.BlockSpec(memory_space=pltpu.VMEM)
    return pl.pallas_call(
        kernel,
        out_shape=out_shapes,
        in_specs=[vmem] * len(args),
        out_specs=jax.tree.map(lambda _: vmem, out_shapes),
        compiler_params=pltpu.CompilerParams(vmem_limit_bytes=VMEM_LIMIT),
        cost_estimate=pl.CostEstimate(flops=flops, transcendentals=0, bytes_accessed=1 << 20),
    )(*args)


def stage_kernel(key_far, value_far, key_here, value_here, sems):
    copies = [
        pltpu.make_async_copy(far, here, sems.at[i])
        for i, (far, here) in enumerate(((key_far, key_here), (value_far, value_here)))
    ]
    for copy in copies:
        copy.start()
    for copy in copies:
        copy.wait()


def stage(keys, values):
    vmem = pl.BlockSpec(memory_space=pltpu.VMEM)
    return pl.pallas_call(
        stage_kernel,
        name="stage",
        out_shape=[jax.ShapeDtypeStruct(x.shape, x.dtype) for x in (keys, values)],
        in_specs=[pl.BlockSpec(memory_space=pl.ANY)] * 2,
        out_specs=[vmem] * 2,
        scratch_shapes=[pltpu.SemaphoreType.DMA((2,))],
        compiler_params=pltpu.CompilerParams(vmem_limit_bytes=VMEM_LIMIT),
        cost_estimate=pl.CostEstimate(flops=0, transcendentals=0, bytes_accessed=4 * keys.size),
    )(keys, values)


def merge_kernel(members, part_ref, share_ref, *out_refs):
    own_rows = out_refs[0].shape[0]
    for j, member in enumerate(members):
        value = part_ref[member * own_rows : (member + 1) * own_rows, :]
        value = value + share_ref[j * own_rows : (j + 1) * own_rows, :].astype(jnp.float32)
        out_refs[j][...] = value.astype(out_refs[j].dtype)


def project_kernel(heads, *refs):
    inputs, refs = refs[:heads], refs[heads:]
    blocks, outs = refs[:-4], refs[-4:]
    own_rows = outs[0].shape[0]
    width = inputs[0].shape[1]
    columns = blocks[0].shape[1]
    for m, block in enumerate(blocks):
        value = None
        for k in range(heads):
            term = jnp.dot(
                inputs[k][...], block[k * width : (k + 1) * width, :], preferred_element_type=jnp.float32
            )
            value = term if value is None else value + term
        value = value.astype(jnp.bfloat16)
        for k in range(4):
            outs[k][:, m * columns : (m + 1) * columns] = value[k * own_rows : (k + 1) * own_rows]


def place_kernel(*refs):
    got, out_ref = refs[:4], refs[4]
    columns = got[0].shape[1] // 2
    seq = lax.axis_index("seq")
    pieces = [[g[:, :columns], g[:, columns:]] for g in got]
    here = lax.rem(seq, 2) == 1
    pieces = [[jnp.where(here, b, a) for a, b in zip(pieces[k], pieces[k ^ 1])] for k in range(4)]
    here = lax.rem(lax.div(seq, 4), 2) == 1
    pieces = [[jnp.where(here, b, a) for a, b in zip(pieces[k], pieces[k ^ 2])] for k in range(4)]
    here = lax.rem(lax.div(seq, 2), 2) == 1
    for k in range(4):
        for m in range(2):
            at = ((k // 2) * 4 + m * 2 + k % 2) * columns
            out_ref[:, at : at + columns] = jnp.where(here, pieces[k][m ^ 1], pieces[k][m])


def on_device(queries, keys, values, mask, out_proj):
    seq_size, heads = lax.axis_size("seq"), lax.axis_size("head")
    lines = seq_size // 4
    per_head = lines // heads
    assert per_head == 2
    own_rows = queries.shape[0]
    columns = out_proj.shape[1]
    total_keys = keys.shape[1] * seq_size
    line, head = lax.axis_index("seq") // 4, lax.axis_index("head")

    def move(x, target):
        pairs = []
        for s in range(seq_size):
            for h in range(heads):
                to = target(s // 4, s % 4, h)
                if to is not None:
                    pairs.append((s * heads + h, (to[0] * 4 + to[1]) * heads + to[2]))
        return lax.ppermute(x, BOTH, pairs)

    def pair(x):
        return move(x, lambda z, p, h: (z, p ^ (1 + h % 2), h))

    def other(x):
        return move(x, lambda z, p, h: (z, p ^ (2 - h % 2), h))

    def along(x, k):
        return move(x, lambda z, p, h: (z ^ k, p, h))

    def inside(x, k):
        return move(x, lambda z, p, h: (z ^ (k >> 1), p ^ (k & 1), h))

    def across(x, k):
        return move(x, lambda z, p, h: (z, p, h ^ k))

    key_own, value_own = keys[0], values[0]
    lined = [queries] + [along(queries, k) for k in range(1, lines)]
    bias = jnp.where(mask > 0, jnp.float32(math.log(total_keys) * LOG2E), jnp.float32(1e30))
    bias_pair, key_pair, value_pair = pair(bias), pair(key_own), pair(value_own)
    q_own = jnp.concatenate(lined, axis=0)
    q_other = other(q_own)

    held, step = [out_proj], 2
    while step < lines:
        held += [along(block, step) for block in held]
        step *= 2
    bit = 1
    while bit < heads:
        here = ((line // 2) ^ head) // bit % 2 == 1
        held = [jnp.where(here, held[i ^ bit], held[i]) for i in range(heads)]
        bit *= 2
    rows_all = jnp.concatenate([held[0]] + [across(held[k], k) for k in range(1, heads)], axis=0)
    proj = [rows_all, move(rows_all, lambda z, p, h: (z, p ^ 2, h))]

    near, far = (bias, *stage(key_own, value_own)), (bias_pair, key_pair, value_pair)

    def attention(q, sources, flip, members, acc=None, dtype=jnp.float32):
        return attend(q, sources, own_rows, flip, members, acc, dtype)

    every, upper, lower = range(lines), range(lines // 2, lines), range(lines // 2)
    part = attention(q_own, [near], (0, 0), every)
    share_upper = attention(q_other, [near, far], (2, 1), upper, dtype=jnp.bfloat16)
    share_upper = other(share_upper)
    share_lower = attention(q_other, [near, far], (2, 1), lower, dtype=jnp.bfloat16)
    share_lower = other(share_lower)
    part = attention(q_own, [far], (0, 0), every, part)
    width = part.shape[1]

    def merge(share, members):
        shapes = [jax.ShapeDtypeStruct((own_rows, width), jnp.bfloat16 if m else jnp.float32) for m in members]
        return small_call(functools.partial(merge_kernel, members), shapes, [part, share])

    merged = merge(share_upper, upper)
    merged = merge(share_lower, lower) + merged
    sums = merged[0]
    for k in range(1, lines):
        sums = sums + along(merged[k], k).astype(jnp.float32)
    attended = sums.astype(jnp.bfloat16)

    quad = jnp.concatenate([attended] + [inside(attended, k) for k in range(1, 4)], axis=0)
    full = [quad] + [across(quad, k) for k in range(1, heads)]
    piece = jax.ShapeDtypeStruct((own_rows, per_head * columns), jnp.bfloat16)
    result = small_call(
        functools.partial(project_kernel, heads),
        [piece] * 4,
        full + proj,
        flops=8 * own_rows * heads * width * per_head * columns,
    )
    got = [result[0]] + [inside(result[k], k) for k in range(1, 4)]
    return small_call(place_kernel, jax.ShapeDtypeStruct((own_rows, 4 * per_head * columns), jnp.bfloat16), got)


def solution(mesh):
    placed = (
        P("seq", "head"),
        P("head", "seq", None),
        P("head", "seq", None),
        P(None, "seq"),
        P("head", "seq"),
    )

    return jax.shard_map(on_device, mesh=mesh, in_specs=placed, out_specs=P("seq", "head"), check_vma=False)
```

```python
import functools
import math

import jax
import jax.numpy as jnp
from jax import lax
from jax.experimental import pallas as pl
from jax.experimental.pallas import tpu as pltpu
from jax.sharding import PartitionSpec as P


BLK = 128
TILE = 256
VMEM_LIMIT = 24 * 1024 * 1024
LOG2E = math.log2(math.e)
BOTH = ("seq", "head")


def attend_kernel(offset, own_rows, flip, members, sources, has_acc, q_ref, *refs):
    given, refs = refs[: 3 * sources], refs[3 * sources :]
    if has_acc:
        acc_in, refs = refs[0], refs[1:]
    out_ref, stacked, total = refs
    width = q_ref.shape[1]
    cached, head_size = given[1].shape
    group = width // head_size
    part = group * own_rows
    tile = min(TILE, cached)
    scale = -LOG2E / math.sqrt(head_size)
    seq = lax.axis_index("seq")
    plane = lax.rem(seq, 4)
    line = lax.div(seq, 4)
    odd = lax.rem(lax.axis_index("head"), 2)
    plane = plane ^ jnp.where(odd == 1, flip[1], flip[0])
    for j, member in enumerate(members):
        for i in range(group):
            stacked[j * part + i * own_rows : j * part + (i + 1) * own_rows, :] = q_ref[
                member * own_rows : (member + 1) * own_rows, i * head_size : (i + 1) * head_size
            ]
    for n in range(sources):
        mask_ref, k_ref, v_ref = given[3 * n : 3 * n + 3]
        biases = []
        for member in members:
            mask_row = ((line ^ member) * 4 + plane) * own_rows // BLK
            live = mask_ref[pl.ds(mask_row, 1), :] > 0
            biases.append(jnp.where(live, offset, 1e30).astype(jnp.float32))
        for t in range(cached // tile):
            score = lax.dot_general(
                stacked[...],
                k_ref[t * tile : (t + 1) * tile, :],
                (((1,), (1,)), ((), ())),
                preferred_element_type=jnp.float32,
            )
            weights = []
            for j in range(len(members)):
                bias = jnp.concatenate(
                    [
                        jnp.broadcast_to(biases[j][:, c : c + 1], (1, BLK))
                        for c in range(t * (tile // BLK), (t + 1) * (tile // BLK))
                    ],
                    axis=1,
                )
                grown = jnp.exp2(score[j * part : (j + 1) * part] * scale + bias)
                weights.append((1.0 / (1.0 + grown)).astype(jnp.bfloat16))
            weight = jnp.concatenate(weights, axis=0)
            term = jnp.dot(weight, v_ref[t * tile : (t + 1) * tile, :], preferred_element_type=jnp.float32)
            total[...] = term if n == 0 and t == 0 else total[...] + term
    for j in range(len(members)):
        for i in range(group):
            here = (slice(j * own_rows, (j + 1) * own_rows), slice(i * head_size, (i + 1) * head_size))
            value = total[j * part + i * own_rows : j * part + (i + 1) * own_rows, :]
            if has_acc:
                value = value + acc_in[members[j] * own_rows : (members[j] + 1) * own_rows, here[1]]
            out_ref[here] = value.astype(out_ref.dtype)


def attend(q, sources, offset, own_rows, flip, members, acc, dtype):
    width = q.shape[1]
    cached, head_size = sources[0][1].shape
    rows = len(members) * own_rows
    stacked = (rows * width // head_size, head_size)
    scores = stacked[0] * cached * len(sources)
    vmem = pl.BlockSpec(memory_space=pltpu.VMEM)
    args = [q] + [x for source in sources for x in source] + ([] if acc is None else [acc])
    return pl.pallas_call(
        functools.partial(attend_kernel, offset, own_rows, flip, members, len(sources), acc is not None),
        out_shape=jax.ShapeDtypeStruct((rows, width), dtype),
        in_specs=[vmem] * len(args),
        out_specs=vmem,
        scratch_shapes=[pltpu.VMEM(stacked, jnp.bfloat16), pltpu.VMEM(stacked, jnp.float32)],
        compiler_params=pltpu.CompilerParams(vmem_limit_bytes=VMEM_LIMIT),
        cost_estimate=pl.CostEstimate(
            flops=4 * scores * head_size, transcendentals=2 * scores, bytes_accessed=4 * cached * head_size
        ),
    )(*args)


def small_call(kernel, out_shapes, args, flops=0):
    vmem = pl.BlockSpec(memory_space=pltpu.VMEM)
    return pl.pallas_call(
        kernel,
        out_shape=out_shapes,
        in_specs=[vmem] * len(args),
        out_specs=jax.tree.map(lambda _: vmem, out_shapes),
        compiler_params=pltpu.CompilerParams(vmem_limit_bytes=VMEM_LIMIT),
        cost_estimate=pl.CostEstimate(flops=flops, transcendentals=0, bytes_accessed=1 << 20),
    )(*args)


def merge_kernel(part_ref, share_ref, *out_refs):
    own_rows = out_refs[0].shape[0]
    for j, out_ref in enumerate(out_refs):
        rows = slice(j * own_rows, (j + 1) * own_rows)
        out_ref[...] = (part_ref[rows, :] + share_ref[rows, :].astype(jnp.float32)).astype(out_ref.dtype)


def project_kernel(heads, *refs):
    inputs, refs = refs[: 2 * heads], refs[2 * heads :]
    blocks, outs = refs[:-4], refs[-4:]
    own_rows = outs[0].shape[0]
    width = inputs[0].shape[1]
    columns = blocks[0].shape[1]
    for m, block in enumerate(blocks):
        value = None
        for k in range(heads):
            rows = jnp.concatenate([inputs[2 * k][...], inputs[2 * k + 1][...]], axis=0)
            term = jnp.dot(rows, block[k * width : (k + 1) * width, :], preferred_element_type=jnp.float32)
            value = term if value is None else value + term
        value = value.astype(jnp.bfloat16)
        for i, k in enumerate((0, 2, 3, 1)):
            outs[k][:, m * columns : (m + 1) * columns] = value[i * own_rows : (i + 1) * own_rows]


def place_kernel(*refs):
    got, out_ref = refs[:4], refs[4]
    columns = got[0].shape[1] // 2
    seq = lax.axis_index("seq")
    pieces = [[g[:, :columns], g[:, columns:]] for g in got]
    here = lax.rem(seq, 2) == 1
    pieces = [[jnp.where(here, b, a) for a, b in zip(pieces[k], pieces[k ^ 1])] for k in range(4)]
    here = lax.rem(lax.div(seq, 4), 2) == 1
    pieces = [[jnp.where(here, b, a) for a, b in zip(pieces[k], pieces[k ^ 2])] for k in range(4)]
    here = lax.rem(lax.div(seq, 2), 2) == 1
    for k in range(4):
        for m in range(2):
            at = ((k // 2) * 4 + m * 2 + k % 2) * columns
            out_ref[:, at : at + columns] = jnp.where(here, pieces[k][m ^ 1], pieces[k][m])


def on_device(queries, keys, values, mask, out_proj):
    seq_size, heads = lax.axis_size("seq"), lax.axis_size("head")
    lines = seq_size // 4
    per_head = lines // heads
    assert per_head == 2
    own_rows = queries.shape[0]
    columns = out_proj.shape[1]
    total_keys = keys.shape[1] * seq_size
    line, head = lax.axis_index("seq") // 4, lax.axis_index("head")

    def move(x, target):
        pairs = []
        for s in range(seq_size):
            for h in range(heads):
                to = target(s // 4, s % 4, h)
                if to is not None:
                    pairs.append((s * heads + h, (to[0] * 4 + to[1]) * heads + to[2]))
        return lax.ppermute(x, BOTH, pairs)

    def pair(x):
        return move(x, lambda z, p, h: (z, p ^ (1 + h % 2), h))

    def other(x):
        return move(x, lambda z, p, h: (z, p ^ (2 - h % 2), h))

    def along(x, k):
        return move(x, lambda z, p, h: (z ^ k, p, h))

    def inside(x, k):
        return move(x, lambda z, p, h: (z ^ (k >> 1), p ^ (k & 1), h))

    def across(x, k):
        return move(x, lambda z, p, h: (z, p, h ^ k))

    key_own, value_own = keys[0], values[0]
    lined = [queries] + [along(queries, k) for k in range(1, lines)]
    offset = math.log(total_keys) * LOG2E
    mask_pair, key_pair, value_pair = pair(mask), pair(key_own), pair(value_own)
    q_own = jnp.concatenate(lined, axis=0)
    q_other = other(q_own)

    held, step = [out_proj], 2
    while step < lines:
        held += [along(block, step) for block in held]
        step *= 2
    bit = 1
    while bit < heads:
        here = ((line // 2) ^ head) // bit % 2 == 1
        held = [jnp.where(here, held[i ^ bit], held[i]) for i in range(heads)]
        bit *= 2
    rows_all = jnp.concatenate([held[0]] + [across(held[k], k) for k in range(1, heads)], axis=0)
    proj = [rows_all, move(rows_all, lambda z, p, h: (z, p ^ 2, h))]

    near, far = (mask, key_own, value_own), (mask_pair, key_pair, value_pair)

    def attention(q, sources, flip, members, acc=None, dtype=jnp.float32):
        return attend(q, sources, offset, own_rows, flip, members, acc, dtype)

    every, upper, lower = range(lines), range(2, lines), range(2)
    part = attention(q_own, [near], (0, 0), every)
    share_upper = attention(q_other, [near, far], (2, 1), upper, dtype=jnp.bfloat16)
    share_upper = other(share_upper)
    part_upper = attention(q_own, [far], (0, 0), upper, part)
    share_lower = attention(q_other, [near, far], (2, 1), lower, dtype=jnp.bfloat16)
    share_lower = other(share_lower)
    part_lower = attention(q_own, [far], (0, 0), lower, part)
    width = part.shape[1]

    def merge(own, share, members):
        shapes = [jax.ShapeDtypeStruct((own_rows, width), jnp.bfloat16 if m % 2 else jnp.float32) for m in members]
        return small_call(merge_kernel, shapes, [own, share])

    merged = merge(part_upper, share_upper, upper)
    passed = along(jnp.concatenate(merged[1::2], axis=0), 1)
    sends = [
        (block + passed[i * own_rows : (i + 1) * own_rows].astype(jnp.float32)).astype(jnp.bfloat16)
        for i, block in enumerate(merged[::2])
    ]
    sums, near_block = merge(part_lower, share_lower, lower)
    for i, block in enumerate(sends):
        sums = sums + along(block, 2 * i + 2).astype(jnp.float32)
    sums = sums + along(near_block, 1).astype(jnp.float32)
    attended = sums.astype(jnp.bfloat16)

    gathered = [inside(attended, k) for k in range(1, 4)]
    groups = [jnp.concatenate([attended, gathered[1], gathered[2]], axis=0), gathered[0]]
    full = [groups] + [[across(g, k) for g in groups] for k in range(1, heads)]
    piece = jax.ShapeDtypeStruct((own_rows, per_head * columns), jnp.bfloat16)
    result = small_call(
        functools.partial(project_kernel, heads),
        [piece] * 4,
        [g for groups in full for g in groups] + proj,
        flops=8 * own_rows * heads * width * per_head * columns,
    )
    got = [result[0]] + [inside(result[k], k) for k in range(1, 4)]
    return small_call(place_kernel, jax.ShapeDtypeStruct((own_rows, 4 * per_head * columns), jnp.bfloat16), got)


def solution(mesh):
    placed = (
        P("seq", "head"),
        P("head", "seq", None),
        P("head", "seq", None),
        P(None, "seq"),
        P("head", "seq"),
    )

    return jax.shard_map(on_device, mesh=mesh, in_specs=placed, out_specs=P("seq", "head"), check_vma=False)
```

```python
import functools
import math

import jax
import jax.numpy as jnp
from jax import lax
from jax.experimental import pallas as pl
from jax.experimental.pallas import tpu as pltpu
from jax.sharding import PartitionSpec as P


BLK = 128
TILE = 256
VMEM_LIMIT = 24 * 1024 * 1024
LOG2E = math.log2(math.e)
BOTH = ("seq", "head")


def attend_kernel(offset, own_rows, flip, members, sources, has_acc, q_ref, *refs):
    given, refs = refs[: 3 * sources], refs[3 * sources :]
    if has_acc:
        acc_in, refs = refs[0], refs[1:]
    out_ref, stacked, total = refs
    width = q_ref.shape[1]
    cached, head_size = given[1].shape
    group = width // head_size
    part = group * own_rows
    tile = min(TILE, cached)
    scale = -LOG2E / math.sqrt(head_size)
    seq = lax.axis_index("seq")
    plane = lax.rem(seq, 4)
    line = lax.div(seq, 4)
    odd = lax.rem(lax.axis_index("head"), 2)
    plane = plane ^ jnp.where(odd == 1, flip[1], flip[0])
    for j, member in enumerate(members):
        for i in range(group):
            stacked[j * part + i * own_rows : j * part + (i + 1) * own_rows, :] = q_ref[
                member * own_rows : (member + 1) * own_rows, i * head_size : (i + 1) * head_size
            ]
    for n in range(sources):
        mask_ref, k_ref, v_ref = given[3 * n : 3 * n + 3]
        biases = []
        for member in members:
            mask_row = ((line ^ member) * 4 + plane) * own_rows // BLK
            live = mask_ref[pl.ds(mask_row, 1), :] > 0
            biases.append(jnp.where(live, offset, 1e30).astype(jnp.float32))
        for t in range(cached // tile):
            score = lax.dot_general(
                stacked[...],
                k_ref[t * tile : (t + 1) * tile, :],
                (((1,), (1,)), ((), ())),
                preferred_element_type=jnp.float32,
            )
            weights = []
            for j in range(len(members)):
                bias = jnp.concatenate(
                    [
                        jnp.broadcast_to(biases[j][:, c : c + 1], (1, BLK))
                        for c in range(t * (tile // BLK), (t + 1) * (tile // BLK))
                    ],
                    axis=1,
                )
                grown = jnp.exp2(score[j * part : (j + 1) * part] * scale + bias)
                weights.append((1.0 / (1.0 + grown)).astype(jnp.bfloat16))
            weight = jnp.concatenate(weights, axis=0)
            term = jnp.dot(weight, v_ref[t * tile : (t + 1) * tile, :], preferred_element_type=jnp.float32)
            total[...] = term if n == 0 and t == 0 else total[...] + term
    for j in range(len(members)):
        for i in range(group):
            here = (slice(j * own_rows, (j + 1) * own_rows), slice(i * head_size, (i + 1) * head_size))
            value = total[j * part + i * own_rows : j * part + (i + 1) * own_rows, :]
            if has_acc:
                value = value + acc_in[here]
            out_ref[here] = value.astype(out_ref.dtype)


def attend(q, sources, offset, own_rows, flip, members, acc, dtype):
    width = q.shape[1]
    cached, head_size = sources[0][1].shape
    rows = len(members) * own_rows
    stacked = (rows * width // head_size, head_size)
    scores = stacked[0] * cached * len(sources)
    vmem = pl.BlockSpec(memory_space=pltpu.VMEM)
    args = [q] + [x for source in sources for x in source] + ([] if acc is None else [acc])
    return pl.pallas_call(
        functools.partial(attend_kernel, offset, own_rows, flip, members, len(sources), acc is not None),
        out_shape=jax.ShapeDtypeStruct((rows, width), dtype),
        in_specs=[vmem] * len(args),
        out_specs=vmem,
        scratch_shapes=[pltpu.VMEM(stacked, jnp.bfloat16), pltpu.VMEM(stacked, jnp.float32)],
        compiler_params=pltpu.CompilerParams(vmem_limit_bytes=VMEM_LIMIT),
        cost_estimate=pl.CostEstimate(
            flops=4 * scores * head_size, transcendentals=2 * scores, bytes_accessed=4 * cached * head_size
        ),
    )(*args)


def small_call(kernel, out_shapes, args, flops=0):
    vmem = pl.BlockSpec(memory_space=pltpu.VMEM)
    return pl.pallas_call(
        kernel,
        out_shape=out_shapes,
        in_specs=[vmem] * len(args),
        out_specs=jax.tree.map(lambda _: vmem, out_shapes),
        compiler_params=pltpu.CompilerParams(vmem_limit_bytes=VMEM_LIMIT),
        cost_estimate=pl.CostEstimate(flops=flops, transcendentals=0, bytes_accessed=1 << 20),
    )(*args)


def merge_kernel(members, part_ref, share_ref, *out_refs):
    own_rows = out_refs[0].shape[0]
    for j, member in enumerate(members):
        value = part_ref[member * own_rows : (member + 1) * own_rows, :]
        value = value + share_ref[j * own_rows : (j + 1) * own_rows, :].astype(jnp.float32)
        out_refs[j][...] = value.astype(out_refs[j].dtype)


def project_kernel(heads, *refs):
    inputs, refs = refs[: 2 * heads], refs[2 * heads :]
    blocks, outs = refs[:-4], refs[-4:]
    own_rows = outs[0].shape[0]
    width = inputs[0].shape[1]
    columns = blocks[0].shape[1]
    for m, block in enumerate(blocks):
        value = None
        for k in range(heads):
            rows = jnp.concatenate([inputs[2 * k][...], inputs[2 * k + 1][...]], axis=0)
            term = jnp.dot(rows, block[k * width : (k + 1) * width, :], preferred_element_type=jnp.float32)
            value = term if value is None else value + term
        value = value.astype(jnp.bfloat16)
        for i, k in enumerate((0, 2, 3, 1)):
            outs[k][:, m * columns : (m + 1) * columns] = value[i * own_rows : (i + 1) * own_rows]


def place_kernel(*refs):
    got, out_ref = refs[:4], refs[4]
    columns = got[0].shape[1] // 2
    seq = lax.axis_index("seq")
    pieces = [[g[:, :columns], g[:, columns:]] for g in got]
    here = lax.rem(seq, 2) == 1
    pieces = [[jnp.where(here, b, a) for a, b in zip(pieces[k], pieces[k ^ 1])] for k in range(4)]
    here = lax.rem(lax.div(seq, 4), 2) == 1
    pieces = [[jnp.where(here, b, a) for a, b in zip(pieces[k], pieces[k ^ 2])] for k in range(4)]
    here = lax.rem(lax.div(seq, 2), 2) == 1
    for k in range(4):
        for m in range(2):
            at = ((k // 2) * 4 + m * 2 + k % 2) * columns
            out_ref[:, at : at + columns] = jnp.where(here, pieces[k][m ^ 1], pieces[k][m])


def on_device(queries, keys, values, mask, out_proj):
    seq_size, heads = lax.axis_size("seq"), lax.axis_size("head")
    lines = seq_size // 4
    per_head = lines // heads
    assert per_head == 2
    own_rows = queries.shape[0]
    columns = out_proj.shape[1]
    total_keys = keys.shape[1] * seq_size
    line, head = lax.axis_index("seq") // 4, lax.axis_index("head")

    def move(x, target):
        pairs = []
        for s in range(seq_size):
            for h in range(heads):
                to = target(s // 4, s % 4, h)
                if to is not None:
                    pairs.append((s * heads + h, (to[0] * 4 + to[1]) * heads + to[2]))
        return lax.ppermute(x, BOTH, pairs)

    def pair(x):
        return move(x, lambda z, p, h: (z, p ^ (1 + h % 2), h))

    def other(x):
        return move(x, lambda z, p, h: (z, p ^ (2 - h % 2), h))

    def along(x, k):
        return move(x, lambda z, p, h: (z ^ k, p, h))

    def inside(x, k):
        return move(x, lambda z, p, h: (z ^ (k >> 1), p ^ (k & 1), h))

    def across(x, k):
        return move(x, lambda z, p, h: (z, p, h ^ k))

    key_own, value_own = keys[0], values[0]
    lined = [queries] + [along(queries, k) for k in range(1, lines)]
    offset = math.log(total_keys) * LOG2E
    mask_pair, key_pair, value_pair = pair(mask), pair(key_own), pair(value_own)
    q_own = jnp.concatenate(lined, axis=0)
    q_other = other(q_own)

    held, step = [out_proj], 2
    while step < lines:
        held += [along(block, step) for block in held]
        step *= 2
    bit = 1
    while bit < heads:
        here = ((line // 2) ^ head) // bit % 2 == 1
        held = [jnp.where(here, held[i ^ bit], held[i]) for i in range(heads)]
        bit *= 2
    rows_all = jnp.concatenate([held[0]] + [across(held[k], k) for k in range(1, heads)], axis=0)
    proj = [rows_all, move(rows_all, lambda z, p, h: (z, p ^ 2, h))]

    near, far = (mask, key_own, value_own), (mask_pair, key_pair, value_pair)

    def attention(q, sources, flip, members, acc=None, dtype=jnp.float32):
        return attend(q, sources, offset, own_rows, flip, members, acc, dtype)

    every, upper, lower = range(lines), range(lines // 2, lines), range(lines // 2)
    part = attention(q_own, [near], (0, 0), every)
    share_upper = attention(q_other, [near, far], (2, 1), upper, dtype=jnp.bfloat16)
    share_upper = other(share_upper)
    share_lower = attention(q_other, [near, far], (2, 1), lower, dtype=jnp.bfloat16)
    share_lower = other(share_lower)
    part = attention(q_own, [far], (0, 0), every, part)
    width = part.shape[1]

    def merge(share, members):
        shapes = [jax.ShapeDtypeStruct((own_rows, width), jnp.bfloat16 if m else jnp.float32) for m in members]
        return small_call(functools.partial(merge_kernel, members), shapes, [part, share])

    merged = merge(share_upper, upper)
    merged = merge(share_lower, lower) + merged
    sums = merged[0]
    for k in range(1, lines):
        sums = sums + along(merged[k], k).astype(jnp.float32)
    attended = sums.astype(jnp.bfloat16)

    gathered = [inside(attended, k) for k in range(1, 4)]
    groups = [jnp.concatenate([attended, gathered[1], gathered[2]], axis=0), gathered[0]]
    full = [groups] + [[across(g, k) for g in groups] for k in range(1, heads)]
    piece = jax.ShapeDtypeStruct((own_rows, per_head * columns), jnp.bfloat16)
    result = small_call(
        functools.partial(project_kernel, heads),
        [piece] * 4,
        [g for groups in full for g in groups] + proj,
        flops=8 * own_rows * heads * width * per_head * columns,
    )
    got = [result[0]] + [inside(result[k], k) for k in range(1, 4)]
    return small_call(place_kernel, jax.ShapeDtypeStruct((own_rows, 4 * per_head * columns), jnp.bfloat16), got)


def solution(mesh):
    placed = (
        P("seq", "head"),
        P("head", "seq", None),
        P("head", "seq", None),
        P(None, "seq"),
        P("head", "seq"),
    )

    return jax.shard_map(on_device, mesh=mesh, in_specs=placed, out_specs=P("seq", "head"), check_vma=False)
```
